32 devices in a mesh: row: 4 (over x, core), col: 8 (over z, y).
Axes of the slice: x: 2, y: 2, z: 4, core: 2. Of those that a mesh axis runs over, the one named last changes fastest.
Arguments:
- w_inter: bfloat16 [3072, 4, 1024], P('col', 'row'), may hold values from -0.109375 to 0.109375
- t_panel: bfloat16 [1024, 4, 3072], P('col', None, 'row'), may hold values from -6 to 6
- amplitudes: float32 [1024, 4, 4, 1024], P('col', None, 'row'), may hold values from -4 to 4
- e_occ: float32 [4], replicated, may hold values from -2 to -0.5
- e_vir: float32 [1024], replicated, may hold values from 0.3 to 3
Outputs:
- new_amplitudes: float32 [1024, 4, 4, 1024], P('col', None, 'row')
The draws below stay inside these ranges and needn't reach their ends.
All inputs are finite; a program needn't handle non-finite values.
Results may differ from the reference program's by a relative error of at most 0.0003.
Values may be sent and summed in bfloat16 or wider, within the bound.
A program may use at most 64 MiB of HBM per device.

```python
import jax
import jax.numpy as jnp

V = 1024
KDIM = 3072
OCC = 4


def steps_of(key, extent, pieces, least, high):
    def one(position, parts):
        draws = jax.random.uniform(jax.random.fold_in(jax.random.fold_in(key, 6), position), (parts,), jnp.float32, least / len(pieces), high / len(pieces))
        return jnp.repeat(jnp.exp(draws), extent[position] // parts).reshape((-1,) + (1,) * (len(extent) - position - 1))

    factor_of = one(*pieces[0])
    for cut in pieces[1:]:
        factor_of = factor_of * one(*cut)
    return factor_of


def scatter_about(rng, shape, scale, most, cuts=(), dtype=jnp.bfloat16):
    factor_of = steps_of(rng, shape, cuts, -0.22, 0.18) if cuts else 1.0
    result = jax.random.normal(rng, shape, jnp.float32) * scale * factor_of
    return jnp.minimum(jnp.maximum(result, -most), most).astype(dtype)


def setup_inputs(seed: int = 0) -> dict:
    splits = jax.random.split(jax.random.key(seed), 6)
    w_inter = scatter_about(splits[0], (KDIM, OCC, V), KDIM ** -0.5, 0.109375, ((0, 8), (1, 4)))
    t_panel = scatter_about(splits[1], (V, OCC, KDIM), 1.0, 6.0, ((0, 8), (2, 4)))
    amplitudes = scatter_about(splits[2], (V, OCC, OCC, V), 0.5, 4.0, ((0, 8), (2, 4)), jnp.float32)
    e_occ = jnp.clip(jax.random.uniform(splits[3], (OCC,), jnp.float32, -2.0, -0.5), -2.0, -0.5)
    e_vir = jnp.clip(jax.random.uniform(splits[4], (V,), jnp.float32, 0.3, 3.0), 0.3, 3.0)
    return dict(w_inter=w_inter, t_panel=t_panel, amplitudes=amplitudes, e_occ=e_occ, e_vir=e_vir)


def reference(w_inter, t_panel, amplitudes, e_occ, e_vir):
    t_matrix = t_panel.reshape(V * OCC, KDIM)
    w_matrix = w_inter.reshape(KDIM, OCC * V)
    contracted = jnp.dot(t_matrix, w_matrix, preferred_element_type=jnp.float32).reshape(V, OCC, OCC, V)
    residual = contracted + jnp.transpose(contracted, (3, 2, 1, 0))
    gaps = (e_occ[None, :, None, None] + e_occ[None, None, :, None]
            - e_vir[:, None, None, None] - e_vir[None, None, None, :])
    return amplitudes + residual / gaps
```

```python
import functools
import math

import jax
import jax.numpy as jnp
from jax import lax
from jax.experimental import pallas as pl
from jax.experimental.pallas import tpu as pltpu
from jax.sharding import PartitionSpec as P

MESH = pl.DeviceIdType.MESH
POWER = 7
LARGEST_T = 6.0
LARGEST_W = 0.109375


def coded(x, scale):
    x = x * scale
    x2 = x * x
    return (x2 * x2 * x2 * x).astype(jnp.bfloat16)


def decoded(y, scale):
    y = y.astype(jnp.float32)
    size = jnp.abs(y)
    root = jnp.exp2(jnp.log2(jnp.maximum(size, 1e-37)) * (1.0 / POWER)) * (1.0 / scale)
    root = jnp.where(size < 1e-37, 0.0, root)
    return jnp.where(y < 0, -root, root)


def kernel(
    rows, height, scale,
    w_ref, t_ref, out_ref,
    w_all, t_all, acc, enc, mirror, direct_out, direct_in,
    local_sem, w_swap, w_send, w_recv, t_send, t_recv, t_core_send, t_core_recv, m_send, m_recv, d_sem,
):
    r = lax.axis_index("row")
    c = lax.axis_index("col")
    hi, lo = c // 2, c % 2
    other = 1 - lo
    quads = rows // 2
    core, quad = r % 2, r // 2
    core_partner = r + 1 - 2 * core
    lo_partner = 2 * hi + other
    peers = rows * height
    me = r * height + hi
    occ = out_ref.shape[0]
    vd = out_ref.shape[1]

    barrier = pltpu.get_barrier_semaphore()

    def greet(d, carry):
        peer = lax.rem(me + d, peers)
        pl.semaphore_signal(barrier, inc=1, device_id=(peer // height, 2 * (peer % height) + lo), device_id_type=MESH)
        return carry

    lax.fori_loop(1, peers, greet, 0)
    pl.semaphore_signal(barrier, inc=1, device_id=(r, lo_partner), device_id_type=MESH)

    w_local = pltpu.make_async_copy(w_ref.at[lo], w_all.at[hi, lo], local_sem.at[0])
    t_local = pltpu.make_async_copy(t_ref, t_all.at[lo, r], local_sem.at[1])
    w_local.start()
    t_local.start()
    pl.semaphore_wait(barrier, peers)

    swap = pltpu.make_async_remote_copy(
        w_ref.at[other], w_all.at[hi, lo], w_swap.at[0], w_swap.at[1], device_id=(r, lo_partner), device_id_type=MESH)
    swap_in = pltpu.make_async_remote_copy(
        w_ref.at[other], w_all.at[hi, other], w_swap.at[0], w_swap.at[1], device_id=(r, lo_partner), device_id_type=MESH)

    def line_copy(way, step, sub, block):
        target = hi + 1 if way == 0 else hi - 1
        half = lo if sub == 0 else other
        source = w_ref.at[lo] if (step == 0 and sub == 0) else w_all.at[block, half]
        return pltpu.make_async_remote_copy(
            source, w_all.at[block, half], w_send.at[way, step, sub], w_recv.at[way, step, sub],
            device_id=(r, 2 * target + lo), device_id_type=MESH)

    def sends(way, step):
        if way == 0:
            return jnp.logical_and(hi + 1 < height, hi - step >= 0)
        return jnp.logical_and(hi >= 1, hi + step < height)

    def receives(way, step):
        return hi - 1 - step >= 0 if way == 0 else hi + 1 + step < height

    def send_line(way, step, sub):
        @pl.when(sends(way, step))
        def _():
            line_copy(way, step, sub, hi - step if way == 0 else hi + step).start()

    def wait_line(way, step, sub):
        @pl.when(receives(way, step))
        def _():
            line_copy(way, step, sub, hi - 1 - step if way == 0 else hi + 1 + step).wait_recv()

    def t_copy(which, source_r, target_r, target_c, send, recv):
        return pltpu.make_async_remote_copy(
            t_all.at[which, source_r], t_all.at[which, source_r], send, recv,
            device_id=(target_r, target_c), device_id_type=MESH)

    def t_row(k, d):
        which = lo if k == 0 else other
        target = 2 * lax.rem(quad + d, quads) + core
        source = t_ref if k == 0 else t_all.at[which, r]
        return pltpu.make_async_remote_copy(
            source, t_all.at[which, r], t_send.at[k, d], t_recv.at[k, d],
            device_id=(target, c), device_id_type=MESH)

    def t_row_in(k, d):
        which = lo if k == 0 else other
        source_r = 2 * lax.rem(quad + quads - d, quads) + core
        return source_r, t_copy(which, source_r, r, c, t_send.at[k, d], t_recv.at[k, d])

    def t_core(k, d, source_r, incoming=False):
        which = lo if k == 0 else other
        return t_copy(which, source_r, core_partner, c, t_core_send.at[k, d], t_core_recv.at[k, d])

    t_lo = pltpu.make_async_remote_copy(
        t_ref, t_all.at[lo, r], t_send.at[0, 0], t_recv.at[0, 0], device_id=(r, lo_partner), device_id_type=MESH)
    t_lo_in = t_copy(other, r, r, lo_partner, t_send.at[0, 0], t_recv.at[0, 0])

    swap.start()
    send_line(0, 0, 0)
    send_line(1, 0, 0)
    for d in range(1, quads):
        t_row(0, d).start()
    t_lo.start()
    t_local.wait()
    t_core(0, 0, r).start()
    w_local.wait()
    swap_in.wait_recv()
    send_line(0, 0, 1)
    send_line(1, 0, 1)

    def relay(step):
        for sub in range(2):
            for way in range(2):
                wait_line(way, step, sub)
                send_line(way, step + 1, sub)

    if height > 2:
        relay(0)
    for d in range(1, quads):
        source_r, copy = t_row_in(0, d)
        copy.wait_recv()
        t_core(0, d, source_r).start()
    t_lo_in.wait_recv()
    t_core(1, 0, r).start()
    for d in range(1, quads):
        t_row(1, d).start()
    for step in range(1, height - 2):
        relay(step)
    for d in range(1, quads):
        source_r, copy = t_row_in(1, d)
        copy.wait_recv()
        t_core(1, d, source_r).start()
    for k in range(2):
        for d in range(quads):
            source_r = 2 * lax.rem(quad + quads - d, quads) + 1 - core
            t_core(k, d, source_r).wait_recv()

    tile = min(256, t_ref.shape[0])
    tiles = t_ref.shape[0] // tile

    def multiply(block, first):
        weights = w_all.at[block]

        def body(n, carry):
            which, place = n // tiles, n % tiles
            at = pl.ds(pl.multiple_of(place * tile, tile), tile)
            left = t_all[which, block, at, :]
            right = jnp.concatenate([weights[0], weights[1]], axis=0)
            product = jnp.dot(left, right, preferred_element_type=jnp.float32)
            if first:
                acc[which, at, :] = product
            else:
                acc[which, at, :] += product
            return carry

        lax.fori_loop(0, 2 * tiles, body, 0)

    multiply(hi, True)
    for step in range(height - 1):
        for way in range(2):
            if step == height - 2:
                wait_line(way, step, 0)
                wait_line(way, step, 1)

            @pl.when(receives(way, step))
            def _():
                multiply(hi - 1 - step if way == 0 else hi + 1 + step, False)

    def code_mirror(n, carry):
        y, j = n // occ, n % occ
        at = pl.ds(pl.multiple_of(j * vd, vd), vd)
        values = coded(acc[y, at, :], scale)
        for z in range(height):
            enc[z, j, y] = values[:, z * vd:(z + 1) * vd]
        direct_out[y, at, :] = values
        return carry

    lax.fori_loop(0, 2 * occ, code_mirror, 0)

    own = pltpu.make_async_copy(enc.at[hi, r], mirror.at[r, hi], local_sem.at[0])
    own.start()

    def mirror_copy(d):
        peer = lax.rem(me + d, peers)
        pr, pz = peer // height, peer % height
        return pltpu.make_async_remote_copy(
            enc.at[pz, pr], mirror.at[r, hi], m_send.at[d], m_recv.at[d],
            device_id=(pr, 2 * pz + lo), device_id_type=MESH)

    def mirror_in(d):
        peer = lax.rem(me + peers - d, peers)
        pr, pz = peer // height, peer % height
        return pr, pz, pltpu.make_async_remote_copy(
            enc.at[pz, pr], mirror.at[pr, pz], m_send.at[d], m_recv.at[d],
            device_id=(pr, 2 * pz + lo), device_id_type=MESH)

    def send_mirror(d, carry):
        mirror_copy(d).start()
        return carry

    lax.fori_loop(1, peers, send_mirror, 0)
    direct = pltpu.make_async_remote_copy(
        direct_out.at[other], direct_in, d_sem.at[0], d_sem.at[1], device_id=(r, lo_partner), device_id_type=MESH)
    direct.start()

    swap.wait_send()
    t_lo.wait_send()
    for step in range(height - 1):
        for way in range(2):
            @pl.when(sends(way, step))
            def _():
                for sub in range(2):
                    line_copy(way, step, sub, hi - step if way == 0 else hi + step).wait_send()
    for k in range(2):
        for d in range(1, quads):
            t_row(k, d).wait_send()
        for d in range(quads):
            t_core(k, d, r).wait_send()

    own.wait()

    def wait_mirror(d, carry):
        mirror_in(d)[2].wait_recv()
        mirror_copy(d).wait_send()
        return carry

    direct.wait()
    lax.fori_loop(1, peers, wait_mirror, 0)

    def combine(j, carry):
        at = pl.ds(pl.multiple_of(j * vd, vd), vd)
        mine = acc[lo, at, :]
        theirs = decoded(direct_in[at, :], scale)
        for z in range(height):
            span = slice(z * vd, (z + 1) * vd)
            for y in range(2):
                here = jnp.where(lo == y, mine[:, span], theirs[:, span])
                there = decoded(mirror[j, z, y], scale)
                col = 2 * z + y
                out_ref[j, :, col * vd:(col + 1) * vd] = here + there.T
        return carry

    lax.fori_loop(0, occ, combine, 0)


def on_device(rows, cols, w_inter, t_panel, amplitudes, e_occ, e_vir):
    row_index = lax.axis_index("row")
    col_index = lax.axis_index("col")
    kw, occ_dev, vir_all = w_inter.shape
    vd, occ, kt = t_panel.shape
    height = cols // 2
    bound = LARGEST_T * LARGEST_W * kw * cols
    scale = 2.0 ** math.floor(119.0 / POWER - math.log2(bound))
    w_half = w_inter.reshape(kw, height, 2, vd).transpose(2, 0, 1, 3).reshape(2, kw, height * vd)
    t_rows = jnp.transpose(t_panel, (1, 0, 2)).reshape(occ * vd, kt)
    half = vir_all // 2
    dma = pltpu.SemaphoreType.DMA
    vmem = pl.BlockSpec(memory_space=pltpu.VMEM)
    residual = pl.pallas_call(
        functools.partial(kernel, rows, height, scale),
        out_shape=jax.ShapeDtypeStruct((occ, vd, vir_all), jnp.float32),
        in_specs=[vmem, vmem],
        out_specs=vmem,
        scratch_shapes=[
            pltpu.VMEM((height, 2, kw, half), jnp.bfloat16),
            pltpu.VMEM((2, rows, occ * vd, kt), jnp.bfloat16),
            pltpu.VMEM((2, occ * vd, half), jnp.float32),
            pltpu.VMEM((height, occ, 2, vd, vd), jnp.bfloat16),
            pltpu.VMEM((occ, height, 2, vd, vd), jnp.bfloat16),
            pltpu.VMEM((2, occ * vd, half), jnp.bfloat16),
            pltpu.VMEM((occ * vd, half), jnp.bfloat16),
            dma((2,)),
            dma((2,)),
            dma((2, height - 1, 2)),
            dma((2, height - 1, 2)),
            dma((2, rows // 2)),
            dma((2, rows // 2)),
            dma((2, rows // 2)),
            dma((2, rows // 2)),
            dma((rows * height,)),
            dma((rows * height,)),
            dma((2,)),
        ],
        compiler_params=pltpu.CompilerParams(
            collective_id=0, has_side_effects=True, vmem_limit_bytes=60 * 1024 * 1024),
        name="amplitude_residual",
    )(w_half, t_rows)
    residual = jnp.transpose(residual, (1, 0, 2))[:, :, None, :]
    occ_mine = lax.dynamic_slice_in_dim(e_occ, row_index * occ_dev, occ_dev)
    vir_mine = lax.dynamic_slice_in_dim(e_vir, col_index * vd, vd)
    gaps = (
        e_occ[None, :, None, None]
        + occ_mine[None, None, :, None]
        - vir_mine[:, None, None, None]
        - e_vir[None, None, None, :]
    )
    return amplitudes + residual / gaps


def solution(mesh):
    rows, cols = mesh.shape["row"], mesh.shape["col"]
    return jax.shard_map(
        functools.partial(on_device, rows, cols),
        mesh=mesh,
        in_specs=(
            P("col", "row", None),
            P("col", None, "row"),
            P("col", None, "row", None),
            P(),
            P(),
        ),
        out_specs=P("col", None, "row", None),
        check_vma=False,
    )
```

```python
import functools
import math

import jax
import jax.numpy as jnp
from jax import lax
from jax.experimental import pallas as pl
from jax.experimental.pallas import tpu as pltpu
from jax.sharding import PartitionSpec as P

MESH = pl.DeviceIdType.MESH
POWER = 7
LARGEST_T = 6.0
LARGEST_W = 0.109375


def coded(x, scale):
    x = x * scale
    x2 = x * x
    return (x2 * x2 * x2 * x).astype(jnp.bfloat16)


def decoded(y, scale):
    y = y.astype(jnp.float32)
    size = jnp.abs(y)
    root = jnp.exp2(jnp.log2(jnp.maximum(size, 1e-37)) * (1.0 / POWER)) * (1.0 / scale)
    root = jnp.where(size < 1e-37, 0.0, root)
    return jnp.where(y < 0, -root, root)


def kernel(
    rows, height, scale,
    w_ref, t_ref, eo_ref, evb_ref, eva_ref, out_ref,
    w_all, w_out, t_all, acc, enc, mirror, direct_out, direct_in, theirs,
    w_sem, local_sem, w_swap, w_send, w_recv, t_send, t_recv, t_core_send, t_core_recv, m_send, m_recv, d_sem,
):
    r = lax.axis_index("row")
    c = lax.axis_index("col")
    hi, lo = c // 2, c % 2
    other = 1 - lo
    quads = rows // 2
    core, quad = r % 2, r // 2
    core_partner = r + 1 - 2 * core
    lo_partner = 2 * hi + other
    peers = rows * height
    me = r * height + hi
    vd = evb_ref.shape[1]
    occ = eo_ref.shape[0]
    kw = w_ref.shape[0]
    half = height * vd
    width = vd if vd % 128 == 0 else half

    def w_columns(buffer, slot, parity):
        copies = []
        for n in range(half // width):
            start = pl.multiple_of((2 * n + parity) * width, 128)
            copies.append(pltpu.make_async_copy(
                w_ref.at[:, pl.ds(start, width)], buffer.at[:, n * width:(n + 1) * width], w_sem.at[slot, n]))
        return copies

    def w_block(block, part):
        return w_all.at[block, pl.ds(pl.multiple_of(part * kw, kw), kw), :]

    w_own = w_columns(w_block(hi, lo), 0, lo)
    w_swap_out = w_columns(w_out, 1, other)
    for copy in w_swap_out + w_own:
        copy.start()

    barrier = pltpu.get_barrier_semaphore()

    def greet(d, carry):
        peer = lax.rem(me + d, peers)
        pl.semaphore_signal(barrier, inc=1, device_id=(peer // height, 2 * (peer % height) + lo), device_id_type=MESH)
        return carry

    lax.fori_loop(1, peers, greet, 0)
    pl.semaphore_signal(barrier, inc=1, device_id=(r, lo_partner), device_id_type=MESH)

    t_local = pltpu.make_async_copy(t_ref, t_all.at[lo, r], local_sem.at[1])
    t_local.start()
    for copy in w_swap_out + w_own:
        copy.wait()
    pl.semaphore_wait(barrier, peers)

    swap = pltpu.make_async_remote_copy(
        w_out, w_block(hi, lo), w_swap.at[0], w_swap.at[1], device_id=(r, lo_partner), device_id_type=MESH)
    swap_in = pltpu.make_async_remote_copy(
        w_out, w_block(hi, other), w_swap.at[0], w_swap.at[1], device_id=(r, lo_partner), device_id_type=MESH)

    def line_copy(way, step, sub, block):
        target = hi + 1 if way == 0 else hi - 1
        part = lo if sub == 0 else other
        return pltpu.make_async_remote_copy(
            w_block(block, part), w_block(block, part), w_send.at[way, step, sub], w_recv.at[way, step, sub],
            device_id=(r, 2 * target + lo), device_id_type=MESH)

    def sends(way, step):
        if way == 0:
            return jnp.logical_and(hi + 1 < height, hi - step >= 0)
        return jnp.logical_and(hi >= 1, hi + step < height)

    def receives(way, step):
        return hi - 1 - step >= 0 if way == 0 else hi + 1 + step < height

    def send_line(way, step, sub):
        @pl.when(sends(way, step))
        def _():
            line_copy(way, step, sub, hi - step if way == 0 else hi + step).start()

    def wait_line(way, step, sub):
        @pl.when(receives(way, step))
        def _():
            line_copy(way, step, sub, hi - 1 - step if way == 0 else hi + 1 + step).wait_recv()

    def t_copy(which, source_r, target_r, target_c, send, recv):
        return pltpu.make_async_remote_copy(
            t_all.at[which, source_r], t_all.at[which, source_r], send, recv,
            device_id=(target_r, target_c), device_id_type=MESH)

    def t_row(k, d):
        which = lo if k == 0 else other
        target = 2 * lax.rem(quad + d, quads) + core
        source = t_ref if k == 0 else t_all.at[which, r]
        return pltpu.make_async_remote_copy(
            source, t_all.at[which, r], t_send.at[k, d], t_recv.at[k, d],
            device_id=(target, c), device_id_type=MESH)

    def t_row_in(k, d):
        which = lo if k == 0 else other
        source_r = 2 * lax.rem(quad + quads - d, quads) + core
        return source_r, t_copy(which, source_r, r, c, t_send.at[k, d], t_recv.at[k, d])

    def t_core(k, d, source_r, incoming=False):
        which = lo if k == 0 else other
        return t_copy(which, source_r, core_partner, c, t_core_send.at[k, d], t_core_recv.at[k, d])

    t_lo = pltpu.make_async_remote_copy(
        t_ref, t_all.at[lo, r], t_send.at[0, 0], t_recv.at[0, 0], device_id=(r, lo_partner), device_id_type=MESH)
    t_lo_in = t_copy(other, r, r, lo_partner, t_send.at[0, 0], t_recv.at[0, 0])

    swap.start()
    send_line(0, 0, 0)
    send_line(1, 0, 0)
    for d in range(1, quads):
        t_row(0, d).start()
    t_lo.start()
    t_local.wait()
    t_core(0, 0, r).start()
    swap_in.wait_recv()
    send_line(0, 0, 1)
    send_line(1, 0, 1)

    def relay(step):
        for sub in range(2):
            for way in range(2):
                wait_line(way, step, sub)
                send_line(way, step + 1, sub)

    if height > 2:
        relay(0)
    for d in range(1, quads):
        source_r, copy = t_row_in(0, d)
        copy.wait_recv()
        t_core(0, d, source_r).start()
    t_lo_in.wait_recv()
    t_core(1, 0, r).start()
    for d in range(1, quads):
        t_row(1, d).start()
    for step in range(1, height - 2):
        relay(step)
    for d in range(1, quads):
        source_r, copy = t_row_in(1, d)
        copy.wait_recv()
        t_core(1, d, source_r).start()
    for k in range(2):
        for d in range(quads):
            source_r = 2 * lax.rem(quad + quads - d, quads) + 1 - core
            t_core(k, d, source_r).wait_recv()

    tile = min(256, t_ref.shape[0])
    tiles = t_ref.shape[0] // tile

    def multiply(block, first):
        def body(n, carry):
            which, place = n // tiles, n % tiles
            at = pl.ds(pl.multiple_of(place * tile, tile), tile)
            left = t_all[which, block, at, :]
            product = jnp.dot(left, w_all[block], preferred_element_type=jnp.float32)
            if first:
                acc[which, at, :] = product
            else:
                acc[which, at, :] += product
            return carry

        lax.fori_loop(0, 2 * tiles, body, 0)

    multiply(hi, True)
    for step in range(height - 1):
        for way in range(2):
            if step == height - 2:
                wait_line(way, step, 0)
                wait_line(way, step, 1)

            @pl.when(receives(way, step))
            def _():
                multiply(hi - 1 - step if way == 0 else hi + 1 + step, False)

    def mirror_copy(pr, pz):
        return pltpu.make_async_remote_copy(
            enc.at[pz, pr], mirror.at[r, hi], m_send.at[pr, pz], m_recv.at[r, hi],
            device_id=(pr, 2 * pz + lo), device_id_type=MESH)

    def mirror_in(pr, pz):
        return pltpu.make_async_remote_copy(
            enc.at[pz, pr], mirror.at[pr, pz], m_send.at[pr, pz], m_recv.at[pr, pz],
            device_id=(pr, 2 * pz + lo), device_id_type=MESH)

    def elsewhere(pr, pz):
        return jnp.logical_or(pr != r, pz != hi)

    own = pltpu.make_async_copy(enc.at[hi, r], mirror.at[r, hi], local_sem.at[0])

    def send_mirror(n, carry):
        j = lax.rem(r + n + 1, occ)
        at = pl.ds(pl.multiple_of(j * vd, vd), vd)
        for y in range(2):
            values = coded(acc[y, at, :], scale)
            for z in range(height):
                enc[z, j, y] = values[:, z * vd:(z + 1) * vd]
            direct_out[y, at, :] = values
        for step in range(height):
            z = jnp.where(2 * hi < height, height - 1 - step, step)

            @pl.when(elsewhere(j, z))
            def _():
                mirror_copy(j, z).start()
        return carry

    lax.fori_loop(0, occ, send_mirror, 0)
    own.start()
    direct = pltpu.make_async_remote_copy(
        direct_out.at[other], direct_in, d_sem.at[0], d_sem.at[1], device_id=(r, lo_partner), device_id_type=MESH)
    direct.start()

    swap.wait_send()
    t_lo.wait_send()
    for step in range(height - 1):
        for way in range(2):
            @pl.when(sends(way, step))
            def _():
                for sub in range(2):
                    line_copy(way, step, sub, hi - step if way == 0 else hi + step).wait_send()
    for k in range(2):
        for d in range(1, quads):
            t_row(k, d).wait_send()
        for d in range(quads):
            t_core(k, d, r).wait_send()

    own.wait()
    direct.wait()

    def decode_direct(j, carry):
        at = pl.ds(pl.multiple_of(j * vd, vd), vd)
        theirs[at, :] = decoded(direct_in[at, :], scale)
        return carry

    lax.fori_loop(0, occ, decode_direct, 0)
    group = max(128 // vd, 1)
    lanes = group * vd
    lines = 2 * half // lanes
    vir_mine = jnp.broadcast_to(evb_ref[pl.ds(c, 1), :], (lanes, vd)).T

    def wait_mirror(pr, pz):
        @pl.when(elsewhere(pr, pz))
        def _():
            mirror_in(pr, pz).wait_recv()

    def combine(n, carry):
        j = lax.rem(n, occ)
        at = pl.ds(pl.multiple_of(j * vd, vd), vd)
        line = n // occ

        def finish(first_z, count):
            for z in range(first_z, first_z + count):
                wait_mirror(j, z)
            blocks = []
            for z in range(first_z, first_z + count):
                span = slice(z * vd, (z + 1) * vd)
                for y in range(2):
                    here = jnp.where(lo == y, acc[lo, at, span], theirs[at, span])
                    blocks.append(here + decoded(mirror[j, z, y], scale).T)
            for start in range(0, len(blocks), group):
                piece = blocks[start:start + group]
                value = piece[0] if group == 1 else jnp.concatenate(piece, axis=1)
                row = (2 * first_z + start) // group
                gaps = (eo_ref[j] + eo_ref[r]) - vir_mine - eva_ref[row:row + 1, :]
                out_ref[pl.ds(j * lines + row, vd, stride=occ * lines), :] = value / gaps

        count = max(group // 2, 1)
        for place in range(height // count):
            @pl.when(line == place)
            def _():
                finish(place * count, count)
        return carry

    count = max(group // 2, 1)
    places = height // count
    here_place = hi // count

    def ordered(n, carry):
        place = lax.rem(here_place + n // occ, places)
        return combine(place * occ + lax.rem(r + n, occ), carry)

    lax.fori_loop(0, places * occ, ordered, 0)

    for pr in range(rows):
        for pz in range(height):
            @pl.when(elsewhere(pr, pz))
            def _():
                mirror_copy(pr, pz).wait_send()


def on_device(rows, cols, w_inter, t_panel, amplitudes, e_occ, e_vir):
    kw, occ_dev, vir_all = w_inter.shape
    vd, occ, kt = t_panel.shape
    height = cols // 2
    bound = LARGEST_T * LARGEST_W * kw * cols
    scale = 2.0 ** math.floor(119.0 / POWER - math.log2(bound))
    w_matrix = w_inter.reshape(kw, vir_all)
    width = vd
    if vd % 128:
        w_matrix = w_matrix.reshape(kw, height, 2, vd).transpose(0, 2, 1, 3).reshape(kw, vir_all)
        width = height * vd
    t_rows = jnp.transpose(t_panel, (1, 0, 2)).reshape(occ * vd, kt)
    half = vir_all // 2
    dma = pltpu.SemaphoreType.DMA
    vmem = pl.BlockSpec(memory_space=pltpu.VMEM)
    lanes = max(128, vd)
    smem = pl.BlockSpec(memory_space=pltpu.SMEM)
    update = pl.pallas_call(
        functools.partial(kernel, rows, height, scale),
        out_shape=jax.ShapeDtypeStruct((vd * occ * vir_all // lanes, lanes), jnp.float32),
        in_specs=[pl.BlockSpec(memory_space=pl.ANY), vmem, smem, vmem, vmem],
        out_specs=vmem,
        scratch_shapes=[
            pltpu.VMEM((height, 2 * kw, half), jnp.bfloat16),
            pltpu.VMEM((kw, half), jnp.bfloat16),
            pltpu.VMEM((2, rows, occ * vd, kt), jnp.bfloat16),
            pltpu.VMEM((2, occ * vd, half), jnp.float32),
            pltpu.VMEM((height, occ, 2, vd, vd), jnp.bfloat16),
            pltpu.VMEM((occ, height, 2, vd, vd), jnp.bfloat16),
            pltpu.VMEM((2, occ * vd, half), jnp.bfloat16),
            pltpu.VMEM((occ * vd, half), jnp.bfloat16),
            pltpu.VMEM((occ * vd, half), jnp.float32),
            dma((2, half // width)),
            dma((2,)),
            dma((2,)),
            dma((2, height - 1, 2)),
            dma((2, height - 1, 2)),
            dma((2, rows // 2)),
            dma((2, rows // 2)),
            dma((2, rows // 2)),
            dma((2, rows // 2)),
            dma((rows, height)),
            dma((rows, height)),
            dma((2,)),
        ],
        compiler_params=pltpu.CompilerParams(
            collective_id=0, has_side_effects=True, vmem_limit_bytes=60 * 1024 * 1024),
        name="amplitude_residual",
    )(w_matrix, t_rows, e_occ, e_vir.reshape(cols, vd), e_vir.reshape(vir_all // lanes, lanes))
    return amplitudes + update.reshape(amplitudes.shape)


def solution(mesh):
    rows, cols = mesh.shape["row"], mesh.shape["col"]
    return jax.shard_map(
        functools.partial(on_device, rows, cols),
        mesh=mesh,
        in_specs=(
            P("col", "row", None),
            P("col", None, "row"),
            P("col", None, "row", None),
            P(),
            P(),
        ),
        out_specs=P("col", None, "row", None),
        check_vma=False,
    )
```

```python
import functools
import math

import jax
import jax.numpy as jnp
from jax import lax
from jax.experimental import pallas as pl
from jax.experimental.pallas import tpu as pltpu
from jax.sharding import PartitionSpec as P

MESH = pl.DeviceIdType.MESH
POWER = 7
LARGEST_T = 6.0
LARGEST_W = 0.109375


def coded(x, scale):
    x = x * scale
    x2 = x * x
    return (x2 * x2 * x2 * x).astype(jnp.bfloat16)


def decoded(y, scale):
    y = y.astype(jnp.float32)
    size = jnp.abs(y)
    root = jnp.exp2(jnp.log2(jnp.maximum(size, 1e-37)) * (1.0 / POWER)) * (1.0 / scale)
    root = jnp.where(size < 1e-37, 0.0, root)
    return jnp.where(y < 0, -root, root)


def kernel(
    rows, height, scale,
    w_ref, t_ref, eo_ref, evb_ref, eva_ref, out_ref,
    w_all, w_out, t_all, acc, enc, mirror, direct_out, direct_in, theirs,
    w_sem, local_sem, w_swap, w_send, w_recv, t_send, t_recv, t_core_send, t_core_recv, m_send, m_recv, d_sem,
):
    r = lax.axis_index("row")
    c = lax.axis_index("col")
    hi, lo = c // 2, c % 2
    other = 1 - lo
    quads = rows // 2
    core, quad = r % 2, r // 2
    core_partner = r + 1 - 2 * core
    lo_partner = 2 * hi + other
    peers = rows * height
    me = r * height + hi
    vd = evb_ref.shape[1]
    occ = eo_ref.shape[0]
    kw = w_ref.shape[0]
    half = height * vd
    width = vd if vd % 128 == 0 else half

    def w_columns(buffer, slot, parity):
        copies = []
        for n in range(half // width):
            start = pl.multiple_of((2 * n + parity) * width, 128)
            copies.append(pltpu.make_async_copy(
                w_ref.at[:, pl.ds(start, width)], buffer.at[:, n * width:(n + 1) * width], w_sem.at[slot, n]))
        return copies

    def w_block(block, part):
        return w_all.at[block, pl.ds(pl.multiple_of(part * kw, kw), kw), :]

    w_own = w_columns(w_block(hi, lo), 0, lo)
    w_swap_out = w_columns(w_out, 1, other)
    for copy in w_swap_out + w_own:
        copy.start()

    barrier = pltpu.get_barrier_semaphore()

    def greet(d, carry):
        peer = lax.rem(me + d, peers)
        pl.semaphore_signal(barrier, inc=1, device_id=(peer // height, 2 * (peer % height) + lo), device_id_type=MESH)
        return carry

    lax.fori_loop(1, peers, greet, 0)
    pl.semaphore_signal(barrier, inc=1, device_id=(r, lo_partner), device_id_type=MESH)

    t_local = pltpu.make_async_copy(t_ref, t_all.at[lo, r], local_sem.at[1])
    t_local.start()
    for copy in w_swap_out + w_own:
        copy.wait()
    pl.semaphore_wait(barrier, peers)

    swap = pltpu.make_async_remote_copy(
        w_out, w_block(hi, lo), w_swap.at[0], w_swap.at[1], device_id=(r, lo_partner), device_id_type=MESH)
    swap_in = pltpu.make_async_remote_copy(
        w_out, w_block(hi, other), w_swap.at[0], w_swap.at[1], device_id=(r, lo_partner), device_id_type=MESH)

    def line_copy(way, step, sub, block):
        target = hi + 1 if way == 0 else hi - 1
        part = lo if sub == 0 else other
        return pltpu.make_async_remote_copy(
            w_block(block, part), w_block(block, part), w_send.at[way, step, sub], w_recv.at[way, step, sub],
            device_id=(r, 2 * target + lo), device_id_type=MESH)

    def sends(way, step):
        if way == 0:
            return jnp.logical_and(hi + 1 < height, hi - step >= 0)
        return jnp.logical_and(hi >= 1, hi + step < height)

    def receives(way, step):
        return hi - 1 - step >= 0 if way == 0 else hi + 1 + step < height

    def send_line(way, step, sub):
        @pl.when(sends(way, step))
        def _():
            line_copy(way, step, sub, hi - step if way == 0 else hi + step).start()

    def wait_line(way, step, sub):
        @pl.when(receives(way, step))
        def _():
            line_copy(way, step, sub, hi - 1 - step if way == 0 else hi + 1 + step).wait_recv()

    def t_copy(which, source_r, target_r, target_c, send, recv):
        return pltpu.make_async_remote_copy(
            t_all.at[which, source_r], t_all.at[which, source_r], send, recv,
            device_id=(target_r, target_c), device_id_type=MESH)

    def t_row(k, d):
        which = lo if k == 0 else other
        target = 2 * lax.rem(quad + d, quads) + core
        source = t_ref if k == 0 else t_all.at[which, r]
        return pltpu.make_async_remote_copy(
            source, t_all.at[which, r], t_send.at[k, d], t_recv.at[k, d],
            device_id=(target, c), device_id_type=MESH)

    def t_row_in(k, d):
        which = lo if k == 0 else other
        source_r = 2 * lax.rem(quad + quads - d, quads) + core
        return source_r, t_copy(which, source_r, r, c, t_send.at[k, d], t_recv.at[k, d])

    def t_core(k, d, source_r, incoming=False):
        which = lo if k == 0 else other
        return t_copy(which, source_r, core_partner, c, t_core_send.at[k, d], t_core_recv.at[k, d])

    t_lo = pltpu.make_async_remote_copy(
        t_ref, t_all.at[lo, r], t_send.at[0, 0], t_recv.at[0, 0], device_id=(r, lo_partner), device_id_type=MESH)
    t_lo_in = t_copy(other, r, r, lo_partner, t_send.at[0, 0], t_recv.at[0, 0])

    swap.start()
    send_line(0, 0, 0)
    send_line(1, 0, 0)
    for d in range(1, quads):
        t_row(0, d).start()
    t_lo.start()
    t_local.wait()
    t_core(0, 0, r).start()
    swap_in.wait_recv()
    send_line(0, 0, 1)
    send_line(1, 0, 1)

    def relay(step):
        for sub in range(2):
            for way in range(2):
                wait_line(way, step, sub)
                send_line(way, step + 1, sub)

    if height > 2:
        relay(0)
    for d in range(1, quads):
        source_r, copy = t_row_in(0, d)
        copy.wait_recv()
        t_core(0, d, source_r).start()
    t_lo_in.wait_recv()
    t_core(1, 0, r).start()
    for d in range(1, quads):
        t_row(1, d).start()
    for step in range(1, height - 2):
        relay(step)
    for d in range(1, quads):
        source_r, copy = t_row_in(1, d)
        copy.wait_recv()
        t_core(1, d, source_r).start()
    for k in range(2):
        for d in range(quads):
            source_r = 2 * lax.rem(quad + quads - d, quads) + 1 - core
            t_core(k, d, source_r).wait_recv()

    tile = min(256, t_ref.shape[0])
    tiles = t_ref.shape[0] // tile

    def multiply(block, first):
        def body(n, carry):
            which, place = n // tiles, n % tiles
            at = pl.ds(pl.multiple_of(place * tile, tile), tile)
            left = t_all[which, block, at, :]
            product = jnp.dot(left, w_all[block], preferred_element_type=jnp.float32)
            if first:
                acc[which, at, :] = product
            else:
                acc[which, at, :] += product
            return carry

        lax.fori_loop(0, 2 * tiles, body, 0)

    multiply(hi, True)
    for step in range(height - 1):
        for way in range(2):
            if step == height - 2:
                wait_line(way, step, 0)
                wait_line(way, step, 1)

            @pl.when(receives(way, step))
            def _():
                multiply(hi - 1 - step if way == 0 else hi + 1 + step, False)

    def mirror_copy(pr, pz):
        return pltpu.make_async_remote_copy(
            enc.at[pz, pr], mirror.at[r, hi], m_send.at[pr, pz], m_recv.at[r, hi],
            device_id=(pr, 2 * pz + lo), device_id_type=MESH)

    def mirror_in(pr, pz):
        return pltpu.make_async_remote_copy(
            enc.at[pz, pr], mirror.at[pr, pz], m_send.at[pr, pz], m_recv.at[pr, pz],
            device_id=(pr, 2 * pz + lo), device_id_type=MESH)

    def elsewhere(pr, pz):
        return jnp.logical_or(pr != r, pz != hi)

    own = pltpu.make_async_copy(enc.at[hi, r], mirror.at[r, hi], local_sem.at[0])

    def send_mirror(n, carry):
        j = lax.rem(r + n + 1, occ)
        at = pl.ds(pl.multiple_of(j * vd, vd), vd)
        for y in range(2):
            values = coded(acc[y, at, :], scale)
            for z in range(height):
                enc[z, j, y] = values[:, z * vd:(z + 1) * vd]
            direct_out[y, at, :] = values
        for step in range(height):
            z = jnp.where(2 * hi < height, height - 1 - step, step)

            @pl.when(elsewhere(j, z))
            def _():
                mirror_copy(j, z).start()
        return carry

    lax.fori_loop(0, occ, send_mirror, 0)
    own.start()
    direct = pltpu.make_async_remote_copy(
        direct_out.at[other], direct_in, d_sem.at[0], d_sem.at[1], device_id=(r, lo_partner), device_id_type=MESH)
    direct.start()

    swap.wait_send()
    t_lo.wait_send()
    for step in range(height - 1):
        for way in range(2):
            @pl.when(sends(way, step))
            def _():
                for sub in range(2):
                    line_copy(way, step, sub, hi - step if way == 0 else hi + step).wait_send()
    for k in range(2):
        for d in range(1, quads):
            t_row(k, d).wait_send()
        for d in range(quads):
            t_core(k, d, r).wait_send()

    own.wait()
    direct.wait()

    def decode_direct(j, carry):
        at = pl.ds(pl.multiple_of(j * vd, vd), vd)
        theirs[at, :] = decoded(direct_in[at, :], scale)
        return carry

    lax.fori_loop(0, occ, decode_direct, 0)
    group = max(128 // vd, 1)
    lanes = group * vd
    lines = 2 * half // lanes
    vir_mine = jnp.broadcast_to(evb_ref[pl.ds(c, 1), :], (lanes, vd)).T

    def wait_mirror(pr, pz):
        @pl.when(elsewhere(pr, pz))
        def _():
            mirror_in(pr, pz).wait_recv()

    def combine(n, carry):
        j = lax.rem(n, occ)
        at = pl.ds(pl.multiple_of(j * vd, vd), vd)
        line = n // occ

        def finish(first_z, count):
            for z in range(first_z, first_z + count):
                wait_mirror(j, z)
            blocks = []
            for z in range(first_z, first_z + count):
                span = slice(z * vd, (z + 1) * vd)
                for y in range(2):
                    here = jnp.where(lo == y, acc[lo, at, span], theirs[at, span])
                    blocks.append(here + decoded(mirror[j, z, y], scale).T)
            for start in range(0, len(blocks), group):
                piece = blocks[start:start + group]
                value = piece[0] if group == 1 else jnp.concatenate(piece, axis=1)
                row = (2 * first_z + start) // group
                gaps = (eo_ref[j] + eo_ref[r]) - vir_mine - eva_ref[row:row + 1, :]
                out_ref[pl.ds(j * lines + row, vd, stride=occ * lines), :] = value / gaps

        count = max(group // 2, 1)
        for place in range(height // count):
            @pl.when(line == place)
            def _():
                finish(place * count, count)
        return carry

    count = max(group // 2, 1)
    places = height // count
    here_place = hi // count

    def ordered(n, carry):
        place = lax.rem(here_place + n // occ, places)
        return combine(place * occ + lax.rem(r + n, occ), carry)

    lax.fori_loop(0, places * occ, ordered, 0)

    for pr in range(rows):
        for pz in range(height):
            @pl.when(elsewhere(pr, pz))
            def _():
                mirror_copy(pr, pz).wait_send()


def on_device(rows, cols, w_inter, t_panel, amplitudes, e_occ, e_vir):
    kw, occ_dev, vir_all = w_inter.shape
    vd, occ, kt = t_panel.shape
    height = cols // 2
    bound = LARGEST_T * LARGEST_W * kw * cols
    scale = 2.0 ** math.floor(119.0 / POWER - math.log2(bound))
    w_matrix = w_inter.reshape(kw, vir_all)
    width = vd
    if vd % 128:
        w_matrix = w_matrix.reshape(kw, height, 2, vd).transpose(0, 2, 1, 3).reshape(kw, vir_all)
        width = height * vd
    t_rows = jnp.transpose(t_panel, (1, 0, 2)).reshape(occ * vd, kt)
    half = vir_all // 2
    dma = pltpu.SemaphoreType.DMA
    vmem = pl.BlockSpec(memory_space=pltpu.VMEM)
    lanes = max(128, vd)
    smem = pl.BlockSpec(memory_space=pltpu.SMEM)
    update = pl.pallas_call(
        functools.partial(kernel, rows, height, scale),
        out_shape=jax.ShapeDtypeStruct((vd * occ * vir_all // lanes, lanes), jnp.float32),
        in_specs=[pl.BlockSpec(memory_space=pl.ANY), vmem, smem, vmem, vmem],
        out_specs=vmem,
        scratch_shapes=[
            pltpu.VMEM((height, 2 * kw, half), jnp.bfloat16),
            pltpu.VMEM((kw, half), jnp.bfloat16),
            pltpu.VMEM((2, rows, occ * vd, kt), jnp.bfloat16),
            pltpu.VMEM((2, occ * vd, half), jnp.float32),
            pltpu.VMEM((height, occ, 2, vd, vd), jnp.bfloat16),
            pltpu.VMEM((occ, height, 2, vd, vd), jnp.bfloat16),
            pltpu.VMEM((2, occ * vd, half), jnp.bfloat16),
            pltpu.VMEM((occ * vd, half), jnp.bfloat16),
            pltpu.VMEM((occ * vd, half), jnp.float32),
            dma((2, half // width)),
            dma((2,)),
            dma((2,)),
            dma((2, height - 1, 2)),
            dma((2, height - 1, 2)),
            dma((2, rows // 2)),
            dma((2, rows // 2)),
            dma((2, rows // 2)),
            dma((2, rows // 2)),
            dma((rows, height)),
            dma((rows, height)),
            dma((2,)),
        ],
        compiler_params=pltpu.CompilerParams(
            collective_id=0, has_side_effects=True, vmem_limit_bytes=60 * 1024 * 1024),
        name="amplitude_residual",
    )(w_matrix, t_rows, e_occ, e_vir.reshape(cols, vd), e_vir.reshape(vir_all // lanes, lanes))
    return (lax.optimization_barrier(amplitudes.reshape(update.shape)) + update).reshape(amplitudes.shape)


def solution(mesh):
    rows, cols = mesh.shape["row"], mesh.shape["col"]
    return jax.shard_map(
        functools.partial(on_device, rows, cols),
        mesh=mesh,
        in_specs=(
            P("col", "row", None),
            P("col", None, "row"),
            P("col", None, "row", None),
            P(),
            P(),
        ),
        out_specs=P("col", None, "row", None),
        check_vma=False,
    )
```
